32 devices in a mesh: tm: 4 (over y, x), space: 8 (over z, core).
Axes of the slice: x: 2, y: 2, z: 4, core: 2. Of those that a mesh axis runs over, the one named last changes fastest.
Arguments:
- starts: float32 [4, 8192, 128], P('tm', 'space'), may hold values from -6 to 6
- volume_op: float32 [128, 128], replicated, may hold values from -0.1875 to 0.1875
- face_lifts: float32 [6, 128, 128], replicated, may hold values from -0.1875 to 0.1875
- neighbours: int32 [8192, 6], P('space'), may hold values from 0 to 8191, as said below
- orientation: int32 [8192, 6], P('space'), may hold values from 0 to 3
Outputs:
- updated: float32 [4, 8192, 128], P('tm', 'space')
The draws below stay inside these ranges and needn't reach their ends.
Inputs may be any that keep to these rules, and one draw needn't show every extreme that they name: neighbours[e, f] lies at most 128 elements from e in the periodic element order, that is it equals (e + k) mod 8192 with -128 <= k <= 128; both k = 128 and k = -128 occur.
All inputs are finite; a program needn't handle non-finite values.
Results may differ from the reference program's by a relative error of at most 0.0001.
Values sent between devices are 32-bit elements; how exact they have to be, the bound alone decides.
A program may use at most 64 MiB of HBM per device.

```python
import jax
import jax.numpy as jnp
from jax import lax

NODES = 128
REACH = 128
STEPS = 4
SLICES = 4
ELEMS = 8192


def draw_neighbours(key, part):
    offsets = jax.random.randint(key, (ELEMS, 6), -REACH, REACH + 1, dtype=jnp.int32)
    row_index = jnp.arange(ELEMS, dtype=jnp.int32)
    at_edge = row_index % 8 == 0
    offsets = offsets.at[:, 0].set(jnp.where(at_edge, REACH, offsets[:, 0]))
    offsets = offsets.at[:, 1].set(jnp.where(at_edge, -REACH, offsets[:, 1]))
    offsets = offsets.at[:, 2].set(jnp.where(row_index % 8 >= 6, 1, offsets[:, 2]))
    return ((row_index[:, None] + offsets) % ELEMS).astype(jnp.int32)


def place_ends(entries, stream_key, smallest, largest):
    dims = entries.shape
    index_at = [jax.random.randint(jax.random.fold_in(stream_key, axis), (), 0, dims[axis]) for axis in range(len(dims))]
    entries = entries.at[tuple(index_at)].set(smallest)
    longest = dims.index(max(dims))
    index_at[longest] = (index_at[longest] + 1) % dims[longest]
    return entries.at[tuple(index_at)].set(largest)


def block_scale(key, dims, shards, least, top_value):
    level = 1.0
    for position, parts in shards:
        heights = jax.random.uniform(jax.random.fold_in(jax.random.fold_in(key, 6), position), (parts,), jnp.float32, least / len(shards), top_value / len(shards))
        level = level * jnp.repeat(jnp.exp(heights), dims[position] // parts).reshape((-1,) + (1,) * (len(dims) - 1 - position))
    return level


def bell_draw(key, shape, scale, reach, shards=(), kind=jnp.bfloat16):
    result = scale * jax.random.normal(key, shape, jnp.float32)
    if shards:
        result = result * block_scale(key, shape, shards, -0.22, 0.18)
    return jnp.clip(result, -reach, reach).astype(kind)


def setup_inputs(seed: int = 0) -> dict:
    key_of = jax.random.split(jax.random.key(seed), 6)
    starts = bell_draw(key_of[0], (SLICES, ELEMS, NODES), 1.0, 6.0, ((0, 4), (1, 8)), jnp.float32)
    volume_op = bell_draw(key_of[1], (NODES, NODES), (7 * NODES) ** -0.5, 0.1875, (), jnp.float32)
    face_lifts = bell_draw(key_of[2], (6, NODES, NODES), (7 * NODES) ** -0.5, 0.1875, (), jnp.float32)
    neighbours = draw_neighbours(jax.random.fold_in(key_of[5], 71), 0)
    orientation = place_ends(jax.random.randint(key_of[4], (ELEMS, 6), 0, 4), jax.random.fold_in(key_of[4], 1), 0, 3).astype(jnp.int32)
    return {"starts": starts, "volume_op": volume_op, "face_lifts": face_lifts, "neighbours": neighbours, "orientation": orientation}


FINE_DT = 0.25
COARSE_DT = 1.0


def twist_rows(gathered, orient_ids):
    node_count = gathered.shape[-1]
    flipped = jnp.where((orient_ids % 2 == 1)[..., None], gathered[..., ::-1], gathered)
    return jnp.where((orient_ids // 2 == 1)[..., None], jnp.roll(flipped, node_count // 2, axis=-1), flipped)


def operate(center, extended, places, orient_ids, volume_op, face_lifts):
    elem_count, node_count = center.shape
    faces = twist_rows(extended[places], orient_ids).reshape(elem_count, 6 * node_count)
    flux = jnp.dot(faces, face_lifts.reshape(6 * node_count, node_count), precision=lax.Precision.HIGHEST, preferred_element_type=jnp.float32)
    inner = jnp.dot(center, volume_op, precision=lax.Precision.HIGHEST, preferred_element_type=jnp.float32)
    return inner + flux - center


def reference(starts, volume_op, face_lifts, neighbours, orientation):
    def coarse_map(state):
        return state + COARSE_DT * operate(state, state, neighbours, orientation, volume_op, face_lifts)

    results = []
    previous = None
    for slot_id in range(SLICES):
        fine_state = starts[slot_id]
        for step_idx in range(STEPS):
            fine_state = fine_state + FINE_DT * operate(fine_state, fine_state, neighbours, orientation, volume_op, face_lifts)
        if slot_id == 0:
            current = fine_state
        else:
            current = coarse_map(previous) + (fine_state - coarse_map(starts[slot_id]))
        results.append(current)
        previous = current
    return jnp.stack(results)
```

```python
import functools

import jax
import jax.numpy as jnp
import numpy as np
from jax import lax
from jax.experimental import pallas as pl
from jax.experimental.pallas import tpu as pltpu
from jax.sharding import PartitionSpec as P

REACH = 128
STEPS = 4
FACES = 6
BLOCK = 256
WINDOW = BLOCK + 2 * REACH

FINE = [81 / 256, 108 / 256, 54 / 256, 12 / 256, 1 / 256]
DIFF = [81 / 256, -148 / 256, 54 / 256, 12 / 256, 1 / 256]

MESH = pl.DeviceIdType.MESH
F32 = jnp.float32
BF16 = jnp.bfloat16


def twist_basis(nodes):
    quarter = nodes // 4
    basis = np.zeros((nodes, nodes), np.float32)
    for column in range(nodes):
        kind, rep = divmod(column, quarter)
        flip, turn = kind & 1, kind >> 1
        half = nodes // 2
        for a in range(2):
            for b in range(2):
                row = nodes - 1 - rep if a else rep
                row = (row + half) % nodes if b else row
                basis[row, column] = 0.5 * (-1) ** (flip * a + turn * b)
    return basis


def split(x):
    hi = x.astype(BF16)
    return hi, (x - hi.astype(F32)).astype(BF16)


def pair(x):
    return jnp.concatenate(split(x), axis=-1)


def kernel(
    times, ring, starts, volume, lifts, nbr, orient, basis, basis_t, out,
    got, coded, ybf, hot, signs, weights, there, back, out_edge, in_edge,
    s_send, s_recv, e_send, e_recv,
):
    rows, nodes = starts.shape[1], starts.shape[2]
    blocks = rows // BLOCK
    n = lax.axis_index("tm")
    me = lax.axis_index("space")
    right, left = lax.rem(me + 1, ring), lax.rem(me + ring - 1, ring)

    barrier = pltpu.get_barrier_semaphore()
    for side in (left, right):
        pl.semaphore_signal(barrier, inc=1, device_id={"space": side}, device_id_type=MESH)
    for step in range(1, times):
        pl.semaphore_signal(
            barrier, inc=1, device_id={"tm": lax.rem(n + step, times)}, device_id_type=MESH
        )
    pl.semaphore_wait(barrier, times + 1)

    def start_copy(source, target):
        return pltpu.make_async_remote_copy(
            src_ref=starts.at[0],
            dst_ref=got.at[source],
            send_sem=s_send.at[target],
            recv_sem=s_recv.at[source],
            device_id={"tm": target},
            device_id_type=MESH,
        )

    for back_step in range(times - 1):
        target = times - 1 - back_step

        @pl.when(n < target)
        def _():
            start_copy(n, target).start()

    def operator(a):
        full = jnp.dot(
            basis_t[...],
            jnp.dot(a, basis[...], precision=lax.Precision.HIGHEST, preferred_element_type=F32),
            precision=lax.Precision.HIGHEST,
            preferred_element_type=F32,
        )
        wide = pair(full)
        return jnp.concatenate([wide, wide], axis=0)

    for f in range(FACES):
        weights[f] = operator(lifts[f])
    weights[FACES] = operator(volume[...])
    there[...] = jnp.concatenate([basis[...], basis[...]], axis=0).astype(BF16)
    back[...] = jnp.concatenate([basis_t[...], basis_t[...]], axis=0).astype(BF16)

    total = rows * ring
    lane = lax.broadcasted_iota(jnp.int32, (BLOCK, nodes), 1) // (nodes // 4)
    flip, turn = lane % 2, lane // 2
    column = lax.broadcasted_iota(jnp.int32, (BLOCK, WINDOW), 1)
    local = lax.broadcasted_iota(jnp.int32, (BLOCK, FACES), 0)

    def prepare(b, carry):
        at = pl.ds(pl.multiple_of(b * BLOCK, BLOCK), BLOCK)
        offset = nbr[at, :] - (me * rows + b * BLOCK + local)
        offset = jnp.where(offset > REACH, offset - total, offset)
        offset = jnp.where(offset < -REACH, offset + total, offset)
        place = local + REACH + offset
        kind = orient[at, :]
        for f in range(FACES):
            hot[b, f] = jnp.where(column == place[:, f : f + 1], 1.0, 0.0).astype(BF16)
            o = kind[:, f : f + 1]
            odd = (flip * (o % 2) + turn * (o // 2)) % 2
            signs[b, f] = (1 - 2 * odd).astype(F32).astype(BF16)
        return carry

    lax.fori_loop(0, blocks, prepare, 0)

    def encode(j, source):
        def body(b, carry):
            at = pl.ds(pl.multiple_of(b * BLOCK, BLOCK), BLOCK)
            coded[j, at, :] = jnp.dot(pair(source(at)), there[...], preferred_element_type=F32)
            return carry

        lax.fori_loop(0, blocks, body, 0)

    encode(n, lambda at: starts[0, at, :])

    def arrive(j):
        @pl.when(j < n)
        def _():
            start_copy(j, n).wait_recv()
            encode(j, lambda at: got[j, at, :])

    def forcing(step, at):
        acc = None
        for i in range(STEPS + 1):
            j = step - STEPS + i
            coef = jnp.where(j == 0, FINE[i], DIFF[i]).astype(F32)
            coef = jnp.where(jnp.logical_and(j >= 0, j <= n), coef, 0.0)
            term = coef * coded[jnp.clip(j, 0, n), at, :]
            acc = term if acc is None else acc + term
        return acc

    def edge_copy(step, side):
        return pltpu.make_async_remote_copy(
            src_ref=out_edge.at[step, side],
            dst_ref=in_edge.at[step, 1 - side],
            send_sem=e_send.at[step, side],
            recv_sem=e_recv.at[step, 1 - side],
            device_id={"space": right if side else left},
            device_id_type=MESH,
        )

    last = n + STEPS

    def finish(step, slot, b, y):
        ybf[slot, pl.ds(REACH + b * BLOCK, BLOCK), :] = pair(y)

        @pl.when(step < last)
        def _():
            if b == 0:
                out_edge[step, 0] = y[:REACH]
                edge_copy(step, 0).start()
            if b == blocks - 1:
                out_edge[step, 1] = y[BLOCK - REACH :]
                edge_copy(step, 1).start()

    order = list(range(1, blocks - 1)) + [0, blocks - 1]

    arrive(0)
    for b in order:
        finish(0, 0, b, forcing(0, pl.ds(b * BLOCK, BLOCK)))

    def advance(step, carry):
        now = lax.rem(step, 2)
        before = 1 - now
        arrive(step)
        for place, b in enumerate(order):
            if place == blocks - 2:
                for side in range(2):
                    edge_copy(step - 1, 1 - side).wait_recv()
                    at = REACH + rows if side else 0
                    ybf[before, pl.ds(at, REACH), :] = pair(in_edge[step - 1, side])
            window = ybf[before, pl.ds(b * BLOCK, WINDOW), :]
            acc = jnp.dot(
                ybf[before, pl.ds(REACH + b * BLOCK, BLOCK), :],
                weights[FACES],
                preferred_element_type=F32,
            )
            for f in range(FACES):
                seen = jnp.dot(hot[b, f], window, preferred_element_type=F32).astype(BF16)
                sign = signs[b, f]
                seen = seen * jnp.concatenate([sign, sign], axis=-1)
                acc = acc + jnp.dot(seen, weights[f], preferred_element_type=F32)
            y = acc[:, :nodes] + acc[:, nodes:] + forcing(step, pl.ds(b * BLOCK, BLOCK))
            finish(step, now, b, y)
        for side in range(2):
            edge_copy(step - 1, side).wait_send()
        return carry

    lax.fori_loop(1, last + 1, advance, 0)

    final = lax.rem(last, 2)

    def decode(b, carry):
        at = pl.ds(pl.multiple_of(REACH + b * BLOCK, REACH), BLOCK)
        to = pl.ds(pl.multiple_of(b * BLOCK, BLOCK), BLOCK)
        out[0, to, :] = jnp.dot(ybf[final, at, :], back[...], preferred_element_type=F32)
        return carry

    lax.fori_loop(0, blocks, decode, 0)

    for target in range(1, times):

        @pl.when(n < target)
        def _():
            start_copy(n, target).wait_send()


def solution(mesh):
    times, ring = mesh.shape["tm"], mesh.shape["space"]

    def per_device(starts, volume_op, face_lifts, neighbours, orientation):
        rows, nodes = starts.shape[1], starts.shape[2]
        blocks = rows // BLOCK
        steps = times + STEPS
        basis = jnp.asarray(twist_basis(nodes))
        basis_t = jnp.asarray(twist_basis(nodes).T.copy())
        return pl.pallas_call(
            functools.partial(kernel, times, ring),
            out_shape=jax.ShapeDtypeStruct(starts.shape, F32),
            in_specs=[pl.BlockSpec(memory_space=pltpu.VMEM)] * 7,
            out_specs=pl.BlockSpec(memory_space=pltpu.VMEM),
            scratch_shapes=[
                pltpu.VMEM((times, rows, nodes), F32),
                pltpu.VMEM((times, rows, nodes), F32),
                pltpu.VMEM((2, rows + 2 * REACH, 2 * nodes), BF16),
                pltpu.VMEM((blocks, FACES, BLOCK, WINDOW), BF16),
                pltpu.VMEM((blocks, FACES, BLOCK, nodes), BF16),
                pltpu.VMEM((FACES + 1, 2 * nodes, 2 * nodes), BF16),
                pltpu.VMEM((2 * nodes, nodes), BF16),
                pltpu.VMEM((2 * nodes, nodes), BF16),
                pltpu.VMEM((steps, 2, REACH, nodes), F32),
                pltpu.VMEM((steps, 2, REACH, nodes), F32),
                pltpu.SemaphoreType.DMA((times,)),
                pltpu.SemaphoreType.DMA((times,)),
                pltpu.SemaphoreType.DMA((steps, 2)),
                pltpu.SemaphoreType.DMA((steps, 2)),
            ],
            compiler_params=pltpu.CompilerParams(
                collective_id=0, has_side_effects=True, vmem_limit_bytes=50 * 1024 * 1024
            ),
        )(starts, volume_op, face_lifts, neighbours, orientation, basis, basis_t)

    return jax.shard_map(
        per_device,
        mesh=mesh,
        in_specs=(P("tm", "space", None), P(), P(), P("space", None), P("space", None)),
        out_specs=P("tm", "space", None),
        check_vma=False,
    )
```

```python
import functools

import jax
import jax.numpy as jnp
import numpy as np
from jax import lax
from jax.experimental import pallas as pl
from jax.experimental.pallas import tpu as pltpu
from jax.sharding import PartitionSpec as P

REACH = 128
STEPS = 4
FACES = 6
BLOCK = 256
WINDOW = BLOCK + 2 * REACH

FINE = [81 / 256, 108 / 256, 54 / 256, 12 / 256, 1 / 256]
DIFF = [81 / 256, -148 / 256, 54 / 256, 12 / 256, 1 / 256]

MESH = pl.DeviceIdType.MESH
F32 = jnp.float32
BF16 = jnp.bfloat16


def twist_basis(nodes):
    quarter = nodes // 4
    basis = np.zeros((nodes, nodes), np.float32)
    for column in range(nodes):
        kind, rep = divmod(column, quarter)
        flip, turn = kind & 1, kind >> 1
        half = nodes // 2
        for a in range(2):
            for b in range(2):
                row = nodes - 1 - rep if a else rep
                row = (row + half) % nodes if b else row
                basis[row, column] = 0.5 * (-1) ** (flip * a + turn * b)
    return basis


def split(x):
    hi = x.astype(BF16)
    return hi, (x - hi.astype(F32)).astype(BF16)


def pair(x):
    return jnp.concatenate(split(x), axis=-1)


def kernel(
    times, ring, starts, volume, lifts, nbr, orient, basis_t, out,
    got, coded, state, halves, hot, place, signs, wide, low, out_edge, in_edge,
    s_send, s_recv, e_send, e_recv,
):
    rows, nodes = starts.shape[1], starts.shape[2]
    blocks, tiles = rows // BLOCK, rows // REACH
    n = lax.axis_index("tm")
    me = lax.axis_index("space")
    right, left = lax.rem(me + 1, ring), lax.rem(me + ring - 1, ring)

    barrier = pltpu.get_barrier_semaphore()
    for side in (left, right):
        pl.semaphore_signal(barrier, inc=1, device_id={"space": side}, device_id_type=MESH)
    for step in range(1, times):
        pl.semaphore_signal(
            barrier, inc=1, device_id={"tm": lax.rem(n + step, times)}, device_id_type=MESH
        )
    pl.semaphore_wait(barrier, times + 1)

    order = list(range(1, blocks - 1)) + [0, blocks - 1]
    square = times == 4 and blocks == 4

    def rows_of(b):
        return pl.ds(pl.multiple_of(b * BLOCK, BLOCK), BLOCK)

    def send(source, b, target, own):
        held = starts.at[0] if own else got.at[source]
        return pltpu.make_async_remote_copy(
            src_ref=held.at[rows_of(b)],
            dst_ref=got.at[source, rows_of(b)],
            send_sem=s_send.at[target, source, b],
            recv_sem=s_recv.at[source, b],
            device_id={"tm": target},
            device_id_type=MESH,
        )

    own_hops, passed_hops = [], []
    if square:
        for b in range(blocks):
            own_hops += [(0, 0, b, 1), (0, 0, b, 2), (1, 1, b, 3), (2, 2, b, 3)]
            passed_hops += [(1 if b < 2 else 2, 0, b, 3), (3, 1, b, 2)]
        first = [(0, 1, 0), (2, 2, 0), (1, 1, 0), (3, 2, 0), (2, 1, 0), (0, 2, 0), (3, 1, 0), (1, 2, 0)]

        @pl.when(n == 0)
        def _():
            for b, target, source in first:
                send(source, b, target, True).start()

        for early in (1, 2):

            @pl.when(n == early)
            def _():
                send(early, order[0], 3, True).start()
    else:
        for target in range(times - 1, 0, -1):

            @pl.when(n < target)
            def _():
                for b in order:
                    send(n, b, target, True).start()

    turn_in = basis_t[...].astype(BF16)
    turn_in = jnp.concatenate([turn_in, turn_in], axis=1)

    def rotate(x):
        return lax.dot_general(turn_in, pair(x), (((1,), (1,)), ((), ())), preferred_element_type=F32)

    def operator(a):
        return split(rotate(jnp.dot(turn_in, jnp.concatenate(split(a), axis=0), preferred_element_type=F32)))

    for p in range(FACES // 2):
        h0, l0 = operator(lifts[2 * p])
        h1, l1 = operator(lifts[2 * p + 1])
        high = jnp.concatenate([h0, h1], axis=1)
        wide[p] = jnp.concatenate([high, jnp.concatenate([l0, l1], axis=1)], axis=0)
        low[p] = high
    hv, lv = operator(volume[...])
    wide[FACES // 2] = jnp.concatenate(
        [jnp.concatenate([hv, hv], axis=1), jnp.concatenate([lv, lv], axis=1)], axis=0
    )

    total = rows * ring
    lane = lax.broadcasted_iota(jnp.int32, (FACES, REACH), 1)
    for t in range(tiles):
        at = pl.ds(t * REACH, REACH)
        offset = nbr[:, at] - (me * rows + t * REACH + lane)
        offset = jnp.where(offset > REACH, offset - total, offset)
        offset = jnp.where(offset < -REACH, offset + total, offset)
        place[t] = lane + REACH + offset
        o = orient[:, at]
        signs[t, 0] = (1 - 2 * (o % 2)).astype(F32)
        signs[t, 1] = (1 - 2 * (o // 2)).astype(F32)

    column = lax.broadcasted_iota(jnp.int32, (WINDOW, BLOCK), 0)
    for b in range(blocks):
        for p in range(FACES // 2):
            f = pl.ds(2 * p + 1, 1)
            row = jnp.concatenate([place[2 * b, f, :], place[2 * b + 1, f, :] + REACH], axis=1)
            hot[b, p] = jnp.where(column == row, 1.0, 0.0).astype(BF16)

    for b in range(blocks):
        coded[n, b] = rotate(starts[0, rows_of(b), :])

    def arrive(j, b):
        send(j, b, n, False).wait_recv()
        coded[j, b] = rotate(got[j, rows_of(b), :])

    @pl.when(n > 0)
    def _():
        def body(i, carry):
            b = lax.rem(i + jnp.where(n == 2, blocks // 2, 0), blocks)
            send(0, b, n, False).wait_recv()
            if square:

                @pl.when(jnp.logical_and(n < 3, i < 2))
                def _():
                    send(0, b, 3, False).start()

            coded[0, b] = rotate(got[0, rows_of(b), :])
            return carry

        lax.fori_loop(0, blocks, body, 0)

    if square:
        for later in (1, 2):

            @pl.when(n == later)
            def _():
                for b in order[1:]:
                    send(later, b, 3, True).start()

    def forcing(step, b):
        acc = None
        for i in range(STEPS + 1):
            j = step - STEPS + i
            coef = jnp.where(j == 0, FINE[i], DIFF[i]).astype(F32)
            coef = jnp.where(jnp.logical_and(j >= 0, j <= n), coef, 0.0)
            term = coef * coded[jnp.clip(j, 0, n), b]
            acc = term if acc is None else acc + term
        return acc

    def edge_copy(step, side):
        return pltpu.make_async_remote_copy(
            src_ref=out_edge.at[step, side],
            dst_ref=in_edge.at[step, 1 - side],
            send_sem=e_send.at[step, side],
            recv_sem=e_recv.at[step, 1 - side],
            device_id={"space": right if side else left},
            device_id_type=MESH,
        )

    last = n + STEPS

    def finish(step, slot, b, y):
        both = jnp.concatenate(split(y), axis=0)
        for u in range(2):
            state[slot, 2 * b + 1 + u] = y[:, u * REACH : (u + 1) * REACH]
            halves[slot, 2 * b + 1 + u] = both[:, u * REACH : (u + 1) * REACH]

        @pl.when(step < last)
        def _():
            if b == 0:
                out_edge[step, 0] = y[:, :REACH]
                edge_copy(step, 0).start()
            if b == blocks - 1:
                out_edge[step, 1] = y[:, REACH:]
                edge_copy(step, 1).start()

    quarter = nodes // 4

    def seen(slot, t, f):
        at = place[t, pl.ds(f, 1), :]
        inner = at % REACH
        index = jnp.broadcast_to(inner, (nodes, REACH))
        tile = jnp.broadcast_to(at // REACH, (nodes, REACH))
        flip = signs[t, 0, pl.ds(f, 1), :]
        turn = signs[t, 1, pl.ds(f, 1), :]

        def take(k):
            return jnp.take_along_axis(
                state[slot, t + k], index, axis=1, mode="promise_in_bounds"
            )

        v = jnp.where(tile == 0, take(0), jnp.where(tile == 1, take(1), take(2)))
        return twisted(v, flip, turn)

    def twisted(v, flip, turn):
        return jnp.concatenate(
            [
                v[:quarter],
                v[quarter : 2 * quarter] * flip,
                v[2 * quarter : 3 * quarter] * turn,
                v[3 * quarter :] * (flip * turn),
            ],
            axis=0,
        )

    def seen_block(slot, b, p):
        window = jnp.concatenate([halves[slot, 2 * b + i] for i in range(4)], axis=1)
        v = jnp.dot(window, hot[b, p], preferred_element_type=F32)
        f = pl.ds(2 * p + 1, 1)
        flip, turn = [
            jnp.concatenate([signs[2 * b, i, f, :], signs[2 * b + 1, i, f, :]], axis=1)
            for i in range(2)
        ]
        return tuple(
            twisted(part, flip, turn).astype(BF16) for part in (v[:nodes], v[nodes:])
        )

    for b in order:
        finish(0, 0, b, forcing(0, b))

    def advance(step, carry):
        now = lax.rem(step, 2)
        before = 1 - now
        for position, b in enumerate(order):
            if position == blocks - 2:
                for side in range(2):
                    edge_copy(step - 1, 1 - side).wait_recv()
                    edge = in_edge[step - 1, side]
                    state[before, (tiles + 1) * side] = edge
                    halves[before, (tiles + 1) * side] = jnp.concatenate(split(edge), axis=0)
            own = jnp.concatenate([halves[before, 2 * b + 1], halves[before, 2 * b + 2]], axis=1)
            acc = jnp.dot(wide[FACES // 2], own, preferred_element_type=F32)
            rest = None
            for p in range(FACES // 2):
                parts = [
                    split(
                        jnp.concatenate(
                            [seen(before, 2 * b, 2 * p), seen(before, 2 * b + 1, 2 * p)], axis=1
                        )
                    ),
                    seen_block(before, b, p),
                ]
                high = jnp.concatenate([parts[0][0], parts[1][0]], axis=0)
                tail = jnp.concatenate([parts[0][1], parts[1][1]], axis=0)
                acc = acc + jnp.dot(wide[p], high, preferred_element_type=F32)
                more = jnp.dot(low[p], tail, preferred_element_type=F32)
                rest = more if rest is None else rest + more

            @pl.when(step < n)
            def _():
                arrive(step, b)
                if square:

                    @pl.when(jnp.logical_and(n == 3, step == 1))
                    def _():
                        send(1, b, 2, False).start()

            finish(step, now, b, acc[:nodes] + acc[nodes:] + rest + forcing(step, b))
        for side in range(2):
            edge_copy(step - 1, side).wait_send()
        return carry

    lax.fori_loop(1, last + 1, advance, 0)

    final = lax.rem(last, 2)
    turn_out = basis_t[...].astype(BF16)
    turn_out = jnp.concatenate([turn_out, turn_out], axis=0)

    for t in range(tiles):
        out[0, pl.ds(t * REACH, REACH), :] = jnp.dot(
            pair(jnp.transpose(state[final, t + 1])), turn_out, preferred_element_type=F32
        )

    if square:
        for who in range(times):

            @pl.when(n == who)
            def _():
                for hops, own in ((own_hops, True), (passed_hops, False)):
                    for sender, source, b, target in hops:
                        if sender == who:
                            send(source, b, target, own).wait_send()
    else:
        for target in range(1, times):

            @pl.when(n < target)
            def _():
                for b in order:
                    send(n, b, target, True).wait_send()


def solution(mesh):
    times, ring = mesh.shape["tm"], mesh.shape["space"]

    def per_device(starts, volume_op, face_lifts, neighbours, orientation):
        rows, nodes = starts.shape[1], starts.shape[2]
        blocks, tiles = rows // BLOCK, rows // REACH
        steps = times + STEPS
        basis_t = jnp.asarray(twist_basis(nodes).T.copy())
        return pl.pallas_call(
            functools.partial(kernel, times, ring),
            out_shape=jax.ShapeDtypeStruct(starts.shape, F32),
            in_specs=[pl.BlockSpec(memory_space=pltpu.VMEM)] * 6,
            out_specs=pl.BlockSpec(memory_space=pltpu.VMEM),
            scratch_shapes=[
                pltpu.VMEM((times, rows, nodes), F32),
                pltpu.VMEM((times, blocks, nodes, BLOCK), F32),
                pltpu.VMEM((2, tiles + 2, nodes, REACH), F32),
                pltpu.VMEM((2, tiles + 2, 2 * nodes, REACH), BF16),
                pltpu.VMEM((blocks, FACES // 2, WINDOW, BLOCK), BF16),
                pltpu.VMEM((tiles, FACES, REACH), jnp.int32),
                pltpu.VMEM((tiles, 2, FACES, REACH), F32),
                pltpu.VMEM((FACES // 2 + 1, 2 * nodes, 2 * nodes), BF16),
                pltpu.VMEM((FACES // 2, nodes, 2 * nodes), BF16),
                pltpu.VMEM((steps, 2, nodes, REACH), F32),
                pltpu.VMEM((steps, 2, nodes, REACH), F32),
                pltpu.SemaphoreType.DMA((times, times, blocks)),
                pltpu.SemaphoreType.DMA((times, blocks)),
                pltpu.SemaphoreType.DMA((steps, 2)),
                pltpu.SemaphoreType.DMA((steps, 2)),
            ],
            compiler_params=pltpu.CompilerParams(
                collective_id=0, has_side_effects=True, vmem_limit_bytes=50 * 1024 * 1024
            ),
        )(starts, volume_op, face_lifts, neighbours.T, orientation.T, basis_t)

    return jax.shard_map(
        per_device,
        mesh=mesh,
        in_specs=(P("tm", "space", None), P(), P(), P("space", None), P("space", None)),
        out_specs=P("tm", "space", None),
        check_vma=False,
    )
```

```python
import functools

import jax
import jax.numpy as jnp
import numpy as np
from jax import lax
from jax.experimental import pallas as pl
from jax.experimental.pallas import tpu as pltpu
from jax.sharding import PartitionSpec as P

REACH = 128
STEPS = 4
FACES = 6
BLOCK = 256
WINDOW = BLOCK + 2 * REACH

FINE = [81 / 256, 108 / 256, 54 / 256, 12 / 256, 1 / 256]
DIFF = [81 / 256, -148 / 256, 54 / 256, 12 / 256, 1 / 256]

MESH = pl.DeviceIdType.MESH
F32 = jnp.float32
BF16 = jnp.bfloat16


def twist_basis(nodes):
    quarter = nodes // 4
    basis = np.zeros((nodes, nodes), np.float32)
    for column in range(nodes):
        kind, rep = divmod(column, quarter)
        flip, turn = kind & 1, kind >> 1
        half = nodes // 2
        for a in range(2):
            for b in range(2):
                row = nodes - 1 - rep if a else rep
                row = (row + half) % nodes if b else row
                basis[row, column] = 0.5 * (-1) ** (flip * a + turn * b)
    return basis


def split(x):
    hi = x.astype(BF16)
    return hi, (x - hi.astype(F32)).astype(BF16)


def pair(x):
    return jnp.concatenate(split(x), axis=-1)


def kernel(
    times, ring, starts, volume, lifts, nbr, orient, basis_t, out,
    got, coded, state, halves, hot, place, signs, wide, low, out_edge, in_edge,
    s_send, s_recv, e_send, e_recv,
):
    rows, nodes = starts.shape[1], starts.shape[2]
    blocks, tiles = rows // BLOCK, rows // REACH
    n = lax.axis_index("tm")
    me = lax.axis_index("space")
    right, left = lax.rem(me + 1, ring), lax.rem(me + ring - 1, ring)

    barrier = pltpu.get_barrier_semaphore()
    for side in (left, right):
        pl.semaphore_signal(barrier, inc=1, device_id={"space": side}, device_id_type=MESH)
    for step in range(1, times):
        pl.semaphore_signal(
            barrier, inc=1, device_id={"tm": lax.rem(n + step, times)}, device_id_type=MESH
        )
    pl.semaphore_wait(barrier, times + 1)

    order = list(range(1, blocks - 1)) + [0, blocks - 1]
    square = times == 4 and blocks == 4

    def rows_of(b):
        return pl.ds(pl.multiple_of(b * BLOCK, BLOCK), BLOCK)

    def send(source, b, target, own):
        held = starts.at[0] if own else got.at[source]
        return pltpu.make_async_remote_copy(
            src_ref=held.at[rows_of(b)],
            dst_ref=got.at[source, rows_of(b)],
            send_sem=s_send.at[target, source, b],
            recv_sem=s_recv.at[source, b],
            device_id={"tm": target},
            device_id_type=MESH,
        )

    own_hops, passed_hops = [], []
    if square:
        for b in range(blocks):
            own_hops += [(0, 0, b, 1), (0, 0, b, 2), (1, 1, b, 3), (2, 2, b, 3)]
            passed_hops += [(1 if b < 2 else 2, 0, b, 3), (3, 1, b, 2)]
        first = [(0, 1, 0), (2, 2, 0), (1, 1, 0), (3, 2, 0), (2, 1, 0), (0, 2, 0), (3, 1, 0), (1, 2, 0)]

        @pl.when(n == 0)
        def _():
            for b, target, source in first:
                send(source, b, target, True).start()

        for early in (1, 2):

            @pl.when(n == early)
            def _():
                send(early, order[0], 3, True).start()
    else:
        for target in range(times - 1, 0, -1):

            @pl.when(n < target)
            def _():
                for b in order:
                    send(n, b, target, True).start()

    turn_in = basis_t[...].astype(BF16)
    turn_in = jnp.concatenate([turn_in, turn_in], axis=1)

    def rotate(x):
        return lax.dot_general(turn_in, pair(x), (((1,), (1,)), ((), ())), preferred_element_type=F32)

    def operator(a):
        return split(rotate(jnp.dot(turn_in, jnp.concatenate(split(a), axis=0), preferred_element_type=F32)))

    for p in range(FACES // 2):
        h0, l0 = operator(lifts[2 * p])
        h1, l1 = operator(lifts[2 * p + 1])
        high = jnp.concatenate([h0, h1], axis=1)
        wide[p] = jnp.concatenate([high, jnp.concatenate([l0, l1], axis=1)], axis=0)
        low[p] = high
    hv, lv = operator(volume[...])
    wide[FACES // 2] = jnp.concatenate(
        [jnp.concatenate([hv, hv], axis=1), jnp.concatenate([lv, lv], axis=1)], axis=0
    )

    total = rows * ring
    lane = lax.broadcasted_iota(jnp.int32, (FACES, REACH), 1)
    for t in range(tiles):
        at = pl.ds(t * REACH, REACH)
        offset = nbr[:, at] - (me * rows + t * REACH + lane)
        offset = jnp.where(offset > REACH, offset - total, offset)
        offset = jnp.where(offset < -REACH, offset + total, offset)
        place[t] = lane + REACH + offset
        o = orient[:, at]
        signs[t, 0] = (1 - 2 * (o % 2)).astype(F32)
        signs[t, 1] = (1 - 2 * (o // 2)).astype(F32)

    column = lax.broadcasted_iota(jnp.int32, (WINDOW, BLOCK), 0)
    for b in range(blocks):
        for p in range(FACES // 2):
            f = pl.ds(2 * p + 1, 1)
            row = jnp.concatenate([place[2 * b, f, :], place[2 * b + 1, f, :] + REACH], axis=1)
            hot[b, p] = jnp.where(column == row, 1.0, 0.0).astype(BF16)

    for b in range(blocks):
        coded[n, b] = rotate(starts[0, rows_of(b), :])

    def arrive(j, b):
        send(j, b, n, False).wait_recv()
        coded[j, b] = rotate(got[j, rows_of(b), :])

    @pl.when(n > 0)
    def _():
        def body(i, carry):
            b = lax.rem(i + jnp.where(n == 2, blocks // 2, 0), blocks)
            send(0, b, n, False).wait_recv()
            if square:

                @pl.when(jnp.logical_and(n < 3, i < 2))
                def _():
                    send(0, b, 3, False).start()

            coded[0, b] = rotate(got[0, rows_of(b), :])
            return carry

        lax.fori_loop(0, blocks, body, 0)

    if square:
        for later in (1, 2):

            @pl.when(n == later)
            def _():
                for b in order[1:]:
                    send(later, b, 3, True).start()

    def forcing(step, b):
        acc = None
        for i in range(STEPS + 1):
            j = step - STEPS + i
            coef = jnp.where(j == 0, FINE[i], DIFF[i]).astype(F32)
            held = jnp.logical_and(j >= 0, j <= n)
            if i == STEPS:
                held = jnp.logical_and(held, jnp.logical_or(step >= n, step == 0))
            place_of = jnp.where(held, j, n)
            term = jnp.where(held, coef, 0.0) * coded[place_of, b]
            acc = term if acc is None else acc + term
        return acc

    def edge_copy(step, side):
        return pltpu.make_async_remote_copy(
            src_ref=out_edge.at[step, side],
            dst_ref=in_edge.at[step, 1 - side],
            send_sem=e_send.at[step, side],
            recv_sem=e_recv.at[step, 1 - side],
            device_id={"space": right if side else left},
            device_id_type=MESH,
        )

    last = n + STEPS

    def store(slot, b, y):
        both = jnp.concatenate(split(y), axis=0)
        for u in range(2):
            state[slot, 2 * b + 1 + u] = y[:, u * REACH : (u + 1) * REACH]
            halves[slot, 2 * b + 1 + u] = both[:, u * REACH : (u + 1) * REACH]

    def send_edges(step, slot):
        @pl.when(step < last)
        def _():
            for side in range(2):
                out_edge[step, side] = state[slot, tiles if side else 1]
                edge_copy(step, side).start()

    quarter = nodes // 4

    def seen(slot, t, f):
        at = place[t, pl.ds(f, 1), :]
        inner = at % REACH
        index = jnp.broadcast_to(inner, (nodes, REACH))
        tile = jnp.broadcast_to(at // REACH, (nodes, REACH))
        flip = signs[t, 0, pl.ds(f, 1), :]
        turn = signs[t, 1, pl.ds(f, 1), :]

        def take(k):
            return jnp.take_along_axis(
                state[slot, t + k], index, axis=1, mode="promise_in_bounds"
            )

        v = jnp.where(tile == 0, take(0), jnp.where(tile == 1, take(1), take(2)))
        return twisted(v, flip, turn)

    def twisted(v, flip, turn):
        return jnp.concatenate(
            [
                v[:quarter],
                v[quarter : 2 * quarter] * flip,
                v[2 * quarter : 3 * quarter] * turn,
                v[3 * quarter :] * (flip * turn),
            ],
            axis=0,
        )

    def seen_block(slot, b, p):
        window = jnp.concatenate([halves[slot, 2 * b + i] for i in range(4)], axis=1)
        v = jnp.dot(window, hot[b, p], preferred_element_type=F32)
        f = pl.ds(2 * p + 1, 1)
        flip, turn = [
            jnp.concatenate([signs[2 * b, i, f, :], signs[2 * b + 1, i, f, :]], axis=1)
            for i in range(2)
        ]
        return tuple(
            twisted(part, flip, turn).astype(BF16) for part in (v[:nodes], v[nodes:])
        )

    def apply(slot, b):
        own = jnp.concatenate([halves[slot, 2 * b + 1], halves[slot, 2 * b + 2]], axis=1)
        acc = jnp.dot(wide[FACES // 2], own, preferred_element_type=F32)
        rest = None
        for p in range(FACES // 2):
            parts = [
                split(
                    jnp.concatenate(
                        [seen(slot, 2 * b, 2 * p), seen(slot, 2 * b + 1, 2 * p)], axis=1
                    )
                ),
                seen_block(slot, b, p),
            ]
            high = jnp.concatenate([parts[0][0], parts[1][0]], axis=0)
            tail = jnp.concatenate([parts[0][1], parts[1][1]], axis=0)
            acc = acc + jnp.dot(wide[p], high, preferred_element_type=F32)
            more = jnp.dot(low[p], tail, preferred_element_type=F32)
            rest = more if rest is None else rest + more
        return acc[:nodes] + acc[nodes:] + rest

    for b in order:
        store(0, b, forcing(0, b))
    send_edges(0, 0)

    def advance(step, carry):
        now = lax.rem(step, 2)
        before = 1 - now
        for region in (order[:-2], order[-2:]):
            if region[0] == 0:
                for side in range(2):
                    edge_copy(step - 1, 1 - side).wait_recv()
                    edge = in_edge[step - 1, side]
                    state[before, (tiles + 1) * side] = edge
                    halves[before, (tiles + 1) * side] = jnp.concatenate(split(edge), axis=0)
            made = [apply(before, b) + forcing(step, b) for b in region]
            for b, y in zip(region, made):
                store(now, b, y)

            @pl.when(step < n)
            def _():
                for b in region:
                    arrive(step, b)
                    if square:

                        @pl.when(jnp.logical_and(n == 3, step == 1))
                        def _():
                            send(1, b, 2, False).start()

                    y = jnp.concatenate([state[now, 2 * b + 1], state[now, 2 * b + 2]], axis=1)
                    store(now, b, y + DIFF[STEPS] * coded[step, b])

        send_edges(step, now)
        for side in range(2):
            edge_copy(step - 1, side).wait_send()
        return carry

    lax.fori_loop(1, last + 1, advance, 0)

    final = lax.rem(last, 2)
    turn_out = basis_t[...].astype(BF16)
    turn_out = jnp.concatenate([turn_out, turn_out], axis=0)

    for t in range(tiles):
        out[0, pl.ds(t * REACH, REACH), :] = jnp.dot(
            pair(jnp.transpose(state[final, t + 1])), turn_out, preferred_element_type=F32
        )

    if square:
        for who in range(times):

            @pl.when(n == who)
            def _():
                for hops, own in ((own_hops, True), (passed_hops, False)):
                    for sender, source, b, target in hops:
                        if sender == who:
                            send(source, b, target, own).wait_send()
    else:
        for target in range(1, times):

            @pl.when(n < target)
            def _():
                for b in order:
                    send(n, b, target, True).wait_send()


def solution(mesh):
    times, ring = mesh.shape["tm"], mesh.shape["space"]

    def per_device(starts, volume_op, face_lifts, neighbours, orientation):
        rows, nodes = starts.shape[1], starts.shape[2]
        blocks, tiles = rows // BLOCK, rows // REACH
        steps = times + STEPS
        basis_t = jnp.asarray(twist_basis(nodes).T.copy())
        return pl.pallas_call(
            functools.partial(kernel, times, ring),
            out_shape=jax.ShapeDtypeStruct(starts.shape, F32),
            in_specs=[pl.BlockSpec(memory_space=pltpu.VMEM)] * 6,
            out_specs=pl.BlockSpec(memory_space=pltpu.VMEM),
            scratch_shapes=[
                pltpu.VMEM((times, rows, nodes), F32),
                pltpu.VMEM((times, blocks, nodes, BLOCK), F32),
                pltpu.VMEM((2, tiles + 2, nodes, REACH), F32),
                pltpu.VMEM((2, tiles + 2, 2 * nodes, REACH), BF16),
                pltpu.VMEM((blocks, FACES // 2, WINDOW, BLOCK), BF16),
                pltpu.VMEM((tiles, FACES, REACH), jnp.int32),
                pltpu.VMEM((tiles, 2, FACES, REACH), F32),
                pltpu.VMEM((FACES // 2 + 1, 2 * nodes, 2 * nodes), BF16),
                pltpu.VMEM((FACES // 2, nodes, 2 * nodes), BF16),
                pltpu.VMEM((steps, 2, nodes, REACH), F32),
                pltpu.VMEM((steps, 2, nodes, REACH), F32),
                pltpu.SemaphoreType.DMA((times, times, blocks)),
                pltpu.SemaphoreType.DMA((times, blocks)),
                pltpu.SemaphoreType.DMA((steps, 2)),
                pltpu.SemaphoreType.DMA((steps, 2)),
            ],
            compiler_params=pltpu.CompilerParams(
                collective_id=0, has_side_effects=True, vmem_limit_bytes=50 * 1024 * 1024
            ),
        )(starts, volume_op, face_lifts, neighbours.T, orientation.T, basis_t)

    return jax.shard_map(
        per_device,
        mesh=mesh,
        in_specs=(P("tm", "space", None), P(), P(), P("space", None), P("space", None)),
        out_specs=P("tm", "space", None),
        check_vma=False,
    )
```
